512 devices in a mesh: gx: 32 (over x, z_lo, core), gy: 16 (over z_hi, y).
Axes of the slice: x: 4, y: 4, z: 16 (z_hi: 4, z_lo: 4; z = z_hi * 4 + z_lo), core: 2. Of those that a mesh axis runs over, the one named last changes fastest.
Arguments:
- points: bfloat16 [524288, 64], P(('gx', 'gy')), may hold values from -6 to 6
- pivots: int32 [2, 128], replicated, may hold values from 0 to 1023, as said below
- owners: int32 [2], replicated, may hold values from 0 to 511
- coeffs: float32 [256, 64], replicated, may hold values from -6 to 6
- noise: float32 [524288, 64], P(('gx', 'gy')), may hold values from -4 to 4
Outputs:
- kernel_probes: float32 [524288, 64], P(('gx', 'gy'))
- factor: float32 [524288, 256], P(('gx', 'gy'))
The draws below stay inside these ranges and needn't reach their ends.
Inputs may be any that keep to these rules, and one draw needn't show every extreme that they name: `pivots`: the two rows together hold 256 distinct indices, among them 0 and 1023.
All inputs are finite; a program needn't handle non-finite values.
Results may differ from the reference program's by a relative error of at most 0.0003.
Values may be sent and summed in bfloat16 or wider, within the bound.
A program may use at most 64 MiB of HBM per device.

```python
import jax
import jax.numpy as jnp
from jax import lax

D = 64
PROBE_VECTORS = 64
PIVOTS = 128
KERNEL_SCALE = 32
P_DEV = 1024
N = 524288
RANK = 256
N_GX = 32
N_GY = 16


latent_rank = 8


def draw_pivots(key, part):
    key_inner, key_order = jax.random.split(jax.random.fold_in(key, 17))
    inner = jax.random.permutation(key_inner, jnp.arange(P_DEV - 2, dtype=jnp.int32)) + 1
    chosen = jnp.concatenate([jnp.array([0, P_DEV - 1], dtype=jnp.int32), inner[:2 * PIVOTS - 2].astype(jnp.int32)])
    order = jax.random.permutation(key_order, jnp.arange(2 * PIVOTS, dtype=jnp.int32))
    return chosen[order].reshape(2, PIVOTS)


def draw_points(key, part):
    key_map, key_latent, key_rough = jax.random.split(jax.random.fold_in(key, 29), 3)
    mixing = jax.random.normal(key_map, (latent_rank, D), jnp.float32) / jnp.sqrt(1.0 * D)
    kernel_spread = jnp.sqrt(KERNEL_SCALE / 4.0)
    latent = jax.random.normal(key_latent, (N, latent_rank), jnp.float32) * kernel_spread
    rough_scale = 0.05
    values = jnp.dot(latent, mixing, precision=lax.Precision.HIGHEST)
    values = values + rough_scale * jax.random.normal(key_rough, (N, D), jnp.float32)
    return jnp.clip(values, -6.0, 6.0).astype(jnp.bfloat16)


def block_scale(stream_key, shape, cuts, smallest, largest):
    def one(dim, shards_of):
        heights = jax.random.uniform(jax.random.fold_in(jax.random.fold_in(stream_key, 6), dim), (shards_of,), jnp.float32, smallest / len(cuts), largest / len(cuts))
        return jnp.repeat(jnp.exp(heights), shape[dim] // shards_of).reshape((-1,) + (1,) * (len(shape) - dim - 1))

    loudness = one(*cuts[0])
    for cut in cuts[1:]:
        loudness = loudness * one(*cut)
    return loudness


def scatter_about(own_key, shape, width, bound, cuts=(), held_as=jnp.bfloat16):
    result = width * jax.random.normal(own_key, shape, jnp.float32)
    if cuts:
        result = result * block_scale(own_key, shape, cuts, -0.22, 0.18)
    return jnp.clip(result, -bound, bound).astype(held_as)


def setup_inputs(seed: int = 0) -> dict:
    keys = jax.random.split(jax.random.key(seed), 6)
    points = draw_points(jax.random.fold_in(keys[5], 71), 0)
    pivots = draw_pivots(jax.random.fold_in(keys[5], 71), 0)
    owners = jax.random.randint(keys[2], (2,), 0, N_GX * N_GY).astype(jnp.int32)
    coeffs = scatter_about(keys[3], (RANK, PROBE_VECTORS), 1.0, 6.0, (), jnp.float32)
    noise = scatter_about(keys[4], (N, PROBE_VECTORS), 0.5, 4.0, ((0, 512),), jnp.float32)
    return {"points": points, "pivots": pivots, "owners": owners, "coeffs": coeffs, "noise": noise}


jitter = 0.1
noise_weight = 0.5

def kern(left, right):
    left32 = left.astype(jnp.float32)
    right32 = right.astype(jnp.float32)
    left_square_norm = lax.optimization_barrier(jnp.sum(left32 * left32, axis=1))
    right_square_norm = lax.optimization_barrier(jnp.sum(right32 * right32, axis=1))
    cross_term = jnp.dot(left32.astype(jnp.float32), right32.T.astype(jnp.float32), precision=lax.Precision.HIGHEST, preferred_element_type=jnp.float32)
    return jnp.exp(-(left_square_norm[:, None] + right_square_norm[None, :] - 2.0 * cross_term) / (1.0 * KERNEL_SCALE))

def reference(points, pivots, owners, coeffs, noise):
    block_list = N_GX * N_GY
    hp = lax.Precision.HIGHEST
    solve = jax.scipy.linalg.solve_triangular

    def pick(round_index):
        start = (owners[round_index] * P_DEV).astype(jnp.int32)
        owner_block = lax.dynamic_slice_in_dim(points, start, P_DEV, 0)
        return owner_block[pivots[round_index]]
    first = pick(0)
    second = pick(1)
    ident = jnp.eye(PIVOTS, dtype=jnp.float32)
    chol_one = jnp.linalg.cholesky(kern(first, first) + jitter * ident)
    first_cols = solve(chol_one, kern(points, first).T, lower=True).T
    rows = solve(chol_one, kern(second, first).T, lower=True).T
    chol_two = jnp.linalg.cholesky(kern(second, second) - jnp.dot(rows, rows.T, precision=hp) + jitter * ident)
    residual_cols = kern(points, second) - jnp.dot(first_cols, rows.T, precision=hp)
    second_cols = solve(chol_two, residual_cols.T, lower=True).T
    factor = jnp.concatenate([first_cols, second_cols], axis=1)
    probes = jnp.dot(factor.astype(jnp.float32), coeffs.astype(jnp.float32), precision=hp, preferred_element_type=jnp.float32) + noise
    probe_bf = probes.astype(jnp.bfloat16)

    def one_block(block_index):
        left_block = lax.dynamic_slice_in_dim(points, (block_index * P_DEV).astype(jnp.int32), P_DEV, 0)
        total = jnp.zeros((P_DEV, PROBE_VECTORS), jnp.float32)
        for block_offset in range(-3, 4):
            other = (block_index + block_offset) % block_list * P_DEV
            other = other.astype(jnp.int32)
            right_block = lax.dynamic_slice_in_dim(points, other, P_DEV, 0)
            right_probe = lax.dynamic_slice_in_dim(probe_bf, other, P_DEV, 0)
            tile = kern(left_block, right_block).astype(jnp.bfloat16)
            total = total + jnp.dot(tile.astype(jnp.float32), right_probe.astype(jnp.float32), precision=hp, preferred_element_type=jnp.float32)
        return total
    banded = lax.map(one_block, jnp.arange(block_list, dtype=jnp.int32)).reshape(N, PROBE_VECTORS)
    kernel_probes = banded / jnp.sqrt(1.0 * P_DEV) + noise_weight * probes
    return (kernel_probes, factor)
```

```python
import jax
import jax.numpy as jnp
from jax import lax
from jax.sharding import PartitionSpec as P

PIVOTS = 128
KERNEL_SCALE = 32


jitter = 0.1
noise_weight = 0.5


def spread(value, axis, source):
    kept = jnp.where(lax.axis_index(axis) == source, value, 0).astype(value.dtype)
    return lax.psum(kept, axis)


def passed_along(value, axis, steps):
    count = lax.axis_size(axis)
    pairs = [(source, (source + steps) % count) for source in range(count)]
    return lax.ppermute(value, axis, pairs)


def kern(left, right):
    left_square_norm = jnp.sum(jnp.square(left.astype(jnp.float32)), axis=1)
    right_square_norm = jnp.sum(jnp.square(right.astype(jnp.float32)), axis=1)
    cross_term = jnp.dot(left, right.T, preferred_element_type=jnp.float32)
    return jnp.exp(
        -(left_square_norm[:, None] + right_square_norm[None, :] - 2.0 * cross_term)
        / (1.0 * KERNEL_SCALE)
    )


def shards(points, pivots, owners, coeffs, noise):
    hp = lax.Precision.HIGHEST
    solve = jax.scipy.linalg.solve_triangular
    width = points.shape[1]
    count = points.shape[0]
    ident = jnp.eye(PIVOTS, dtype=jnp.float32)
    first = spread(points[pivots[0]], ("gx", "gy"), owners[0])
    second = spread(points[pivots[1]], ("gx", "gy"), owners[1])
    chol_one = jnp.linalg.cholesky(kern(first, first) + jitter * ident)
    first_cols = solve(chol_one, kern(points, first).T, lower=True).T
    rows = solve(chol_one, kern(second, first).T, lower=True).T
    chol_two = jnp.linalg.cholesky(
        kern(second, second) - jnp.dot(rows, rows.T, precision=hp) + jitter * ident
    )
    residual_cols = kern(points, second) - jnp.dot(first_cols, rows.T, precision=hp)
    second_cols = solve(chol_two, residual_cols.T, lower=True).T
    factor = jnp.concatenate([first_cols, second_cols], axis=1)
    probes = jnp.dot(factor, coeffs, precision=hp, preferred_element_type=jnp.float32) + noise
    packed = jnp.concatenate([points, probes.astype(jnp.bfloat16)], axis=1)

    def contribute(total, piece):
        tile = kern(points, piece[:, :width]).astype(jnp.bfloat16)
        return total + jnp.dot(tile, piece[:, width:], preferred_element_type=jnp.float32)

    total = contribute(jnp.zeros((count, probes.shape[1]), jnp.float32), packed)
    piece = passed_along(packed, ("gx", "gy"), -3)
    total = contribute(total, piece)
    for stop_index in range(5):
        if stop_index == 2:
            piece = passed_along(piece, ("gx", "gy"), 2)
        else:
            piece = passed_along(piece, ("gx", "gy"), 1)
        total = contribute(total, piece)
    kernel_probes = total / jnp.sqrt(1.0 * count) + noise_weight * probes
    return (kernel_probes, factor)


def solution(mesh):
    in_specs = (P(("gx", "gy"), None), P(), P(), P(), P(("gx", "gy"), None))
    out_specs = (P(("gx", "gy"), None), P(("gx", "gy"), None))
    return jax.shard_map(shards, mesh=mesh, in_specs=in_specs, out_specs=out_specs, check_vma=False)
```

```python
import jax
import jax.numpy as jnp
from jax import lax
from jax.experimental import pallas as pl
from jax.experimental.pallas import tpu as pltpu
from jax.sharding import PartitionSpec as P

MESH = pl.DeviceIdType.MESH
F32, BF16 = jnp.float32, jnp.bfloat16
HIGHEST = lax.Precision.HIGHEST

POINTS = 1024
WIDTH = 64
PIVOTS = 128
RANK = 256
SCALE = 32.0
JITTER = 0.1
NOISE_WEIGHT = 0.5
LANES = 128
CHUNK = 128
CHUNKS = POINTS // CHUNK

FIRST_ROUND = (1, 15, 2, 14, 8)
SECOND_ROUND = (5, 11)

SEM_CORE, SEM_Y, SEM_X, SEM_Z, SEM_CORE_BACK = 0, 1, 4, 7, 14
SEM_ZP, SEM_ZN, SEM_OP, SEM_ON, SEM_RP, SEM_RN = 15, 17, 19, 22, 25, 28
SEMS = 31


def dot(a, b, ca=1, cb=0, precision=None):
    return lax.dot_general(
        a, b, (((ca,), (cb,)), ((), ())), precision=precision, preferred_element_type=F32
    )


def three_parts(value):
    high = value.astype(BF16).astype(F32)
    rest = value - high
    middle = rest.astype(BF16).astype(F32)
    return high, middle, rest - middle


def right_columns(points_t):
    count = points_t.shape[1]
    norm = jnp.sum(points_t * points_t, axis=0, keepdims=True) * (-1.0 / SCALE)
    high, middle, low = three_parts(norm)
    row = lax.broadcasted_iota(jnp.int32, (LANES - WIDTH, count), 0)
    extra = jnp.where(row == 0, high, 0.0)
    extra = jnp.where(row == 1, middle, extra)
    extra = jnp.where(row == 2, low, extra)
    extra = jnp.where((row >= 3) & (row < 6), 1.0, extra)
    return extra


def left_columns(points_t):
    count = points_t.shape[1]
    norm = jnp.sum(points_t * points_t, axis=0, keepdims=True) * (-1.0 / SCALE)
    high, middle, low = three_parts(norm)
    row = lax.broadcasted_iota(jnp.int32, (LANES - WIDTH, count), 0)
    extra = jnp.where(row < 3, 1.0, 0.0)
    extra = jnp.where(row == 3, high, extra)
    extra = jnp.where(row == 4, middle, extra)
    extra = jnp.where(row == 5, low, extra)
    return extra


def pivot_rows(value):
    norm = jnp.sum(value * value, axis=1, keepdims=True) * (-1.0 / SCALE)
    high, middle, low = three_parts(norm)
    lane = lax.broadcasted_iota(jnp.int32, value.shape, 1)
    left = value * (2.0 / SCALE)
    left = jnp.where((lane >= 64) & (lane < 67), 1.0, left)
    left = jnp.where(lane == 67, high, left)
    left = jnp.where(lane == 68, middle, left)
    left = jnp.where(lane == 69, low, left)
    right = jnp.where(lane == 64, high, value)
    right = jnp.where(lane == 65, middle, right)
    right = jnp.where(lane == 66, low, right)
    right = jnp.where((lane >= 67) & (lane < 70), 1.0, right)
    return left.astype(BF16), right.astype(BF16)


def inverse_factor(matrix):
    n = PIVOTS
    rows = n // 8
    tiles = [matrix[8 * t : 8 * t + 8, :] for t in range(rows)]
    lane = lax.broadcasted_iota(jnp.int32, (8, n), 1)
    sub = lax.broadcasted_iota(jnp.int32, (8, n), 0)
    for k in range(n):
        top, r = k // 8, k % 8
        pivot_row = jnp.broadcast_to(tiles[top][r : r + 1, :], (8, n))
        pivot = jnp.broadcast_to(tiles[top][r : r + 1, k : k + 1], (8, n))
        scaled = (pivot_row + jnp.where(lane == k, 1.0, 0.0)) * (1.0 / pivot)
        for t in range(top, rows):
            column = jnp.broadcast_to(tiles[t][:, k : k + 1], (8, n))
            if t == top:
                if r == 7:
                    continue
                column = jnp.where(sub > r, column, 0.0)
            tiles[t] = tiles[t] - column * scaled
    out = []
    for t in range(rows):
        diagonal = jnp.sum(jnp.where(lane == sub + 8 * t, tiles[t], 0.0), axis=1, keepdims=True)
        unit = jnp.where(lane < sub + 8 * t, tiles[t], jnp.where(lane == sub + 8 * t, 1.0, 0.0))
        out.append(unit * (1.0 / jnp.sqrt(diagonal)))
    return jnp.concatenate(out, axis=0)


def kernel(
    owners, pivots, points_t, coeffs_t, noise_t, out_t, factor,
    noise_bf, mine, core_buf, stage, y_buf, x_buf, z_buf, pivot_buf, far_points, far_noise,
    near_points, near_noise, left, right, tiles, inverse, probe_bf, probes_t, send, recv,
):
    gx, gy = lax.axis_index("gx"), lax.axis_index("gy")
    core, z_lo, x = gx % 2, (gx // 2) % 4, gx // 8
    z_hi, y = gy // 4, gy % 4
    z = z_hi * 4 + z_lo
    group = gx * 4 + z_hi
    me = gx * 16 + gy

    def at(x, z, core, y):
        return ((x * 4 + z % 4) * 2 + core, (z // 4) * 4 + y)

    def group_at(step):
        other = (group + step + 128) % 128
        return (other // 4, (other % 4) * 4 + y)

    other_core = at(x, z, 1 - core, y)
    y_mates = [at(x, z, core, (y + k) % 4) for k in (1, 2, 3)]
    x_mates = [at((x + k) % 4, z, core, y) for k in (1, 2, 3)]
    z_mates = [at(x, (z + d) % 16, core, y) for d in FIRST_ROUND + SECOND_ROUND]
    after, before = group_at(1), group_at(-1)

    barrier = pltpu.get_barrier_semaphore()
    peers = [other_core] + y_mates + x_mates + z_mates + [after, before]
    for peer in peers:
        pl.semaphore_signal(barrier, inc=1, device_id=peer, device_id_type=MESH)

    def copy(source, target, number, device):
        return pltpu.make_async_remote_copy(
            src_ref=source, dst_ref=target, send_sem=send.at[number], recv_sem=recv.at[number],
            device_id=device, device_id_type=MESH,
        )

    own = points_t[...].astype(F32)
    right[6, 0:WIDTH, :] = points_t[...]
    right[6, WIDTH:, :] = right_columns(own).astype(BF16)
    left[...] = jnp.concatenate([own * (2.0 / SCALE), left_columns(own)], axis=0).T.astype(BF16)
    noise_bf[...] = noise_t[...].astype(BF16)
    index = lax.broadcasted_iota(jnp.int32, (PIVOTS, POINTS), 1)
    for turn in range(2):
        wanted = jnp.where(owners[turn] == me, pivots[turn : turn + 1, :], -1)
        wanted = jnp.broadcast_to(wanted, (PIVOTS, PIVOTS)).T[:, 0:1]
        chosen = jnp.where(index == wanted, 1.0, 0.0).astype(BF16)
        rows = dot(chosen, points_t[...], 1, 1).astype(BF16)
        for half in range(2):
            mine[half, :, WIDTH * turn : WIDTH * (turn + 1)] = rows[64 * half : 64 * half + 64, :]

    pl.semaphore_wait(barrier, len(peers))

    def started(copies):
        for one in copies:
            one.start()
        return copies

    def fill_tile(c, low, high):
        def step(i, carry):
            at_rows = pl.ds(pl.multiple_of(i * CHUNK, CHUNK), CHUNK)
            tiles[c, at_rows, :] = jnp.exp(dot(left[at_rows, :], right[c])).astype(BF16)
            return carry

        lax.fori_loop(low, high, step, 0)

    def fill_right(c):
        block = near_points[c].astype(F32)
        right[c, 0:WIDTH, :] = near_points[c]
        right[c, WIDTH:, :] = right_columns(block).astype(BF16)

    everything = []
    core_copy = started([copy(mine.at[1 - core], core_buf, SEM_CORE, other_core)])
    far_p = started([
        copy(points_t, far_points.at[0], SEM_ZP, after),
        copy(points_t, far_points.at[1], SEM_ZP + 1, before),
    ])
    near_p = started([copy(points_t, near_points.at[k], SEM_OP + k, y_mates[k]) for k in range(3)])
    fill_tile(6, 0, 1)
    core_copy[0].wait_recv()
    stage[0] = mine[core] + core_buf[...]

    x_copies = started([copy(stage.at[0], x_buf.at[k], SEM_X + k, x_mates[k]) for k in range(3)])
    fill_tile(6, 1, 3)
    for one in x_copies:
        one.wait_recv()
    stage[1] = stage[0] + x_buf[0] + x_buf[1] + x_buf[2]

    y_copies = started([copy(stage.at[1], y_buf.at[k], SEM_Y + k, y_mates[k]) for k in range(3)])
    fill_tile(6, 3, 6)
    for one in y_copies:
        one.wait_recv()
    stage[2] = stage[1] + y_buf[0] + y_buf[1] + y_buf[2]

    def either(a, b):
        return jnp.where(a == 0, b, a)

    z_copies = started([
        copy(stage.at[2], z_buf.at[k], SEM_Z + k, z_mates[k]) for k in range(len(FIRST_ROUND))
    ])
    fill_tile(6, 6, 8)
    for k in range(4):
        z_copies[k].wait_recv()
    gathered = stage[2]
    for k in range(4):
        gathered = either(gathered, z_buf[k])
    stage[3] = gathered
    z_more = started([
        copy(stage.at[3], z_buf.at[k], SEM_Z + k, z_mates[k])
        for k in range(len(FIRST_ROUND), len(FIRST_ROUND) + len(SECOND_ROUND))
    ])
    near_n = started([copy(noise_bf, near_noise.at[k], SEM_ON + k, y_mates[k]) for k in range(3)])
    near_p[0].wait_recv()
    fill_right(0)
    fill_tile(0, 0, 4)
    z_copies[4].wait_recv()
    for one in z_more:
        one.wait_recv()
    gathered = stage[3]
    for k in range(4, 7):
        gathered = either(gathered, z_buf[k])
    pivot_buf[core] = gathered
    back = started([copy(pivot_buf.at[core], pivot_buf.at[core], SEM_CORE_BACK, other_core)])
    far_n = started([
        copy(noise_bf, far_noise.at[0], SEM_ZN, after),
        copy(noise_bf, far_noise.at[1], SEM_ZN + 1, before),
    ])
    for one in far_p:
        one.wait_recv()
    which = [1 - (y + k) // 4 for k in (1, 2, 3)]
    relay_p = started([
        copy(far_points.at[which[k]], near_points.at[3 + k], SEM_RP + k, y_mates[k]) for k in range(3)
    ])
    back[0].wait_recv()

    both = jnp.concatenate([pivot_buf[0], pivot_buf[1]], axis=0).astype(F32)
    lane = lax.broadcasted_iota(jnp.int32, both.shape, 1)
    first = jnp.where(lane < WIDTH, both, 0.0)
    second = jnp.where(lane < WIDTH, pltpu.roll(both, WIDTH, 1), 0.0)
    first_left, first_right = pivot_rows(first)
    second_left, second_right = pivot_rows(second)
    square = lax.broadcasted_iota(jnp.int32, (PIVOTS, PIVOTS), 0) == lax.broadcasted_iota(
        jnp.int32, (PIVOTS, PIVOTS), 1
    )
    jitter = jnp.where(square, JITTER, 0.0)
    one_one = jnp.exp(dot(first_left, first_right, 1, 1)) + jitter
    two_one = jnp.exp(dot(second_left, first_right, 1, 1))
    two_two = jnp.exp(dot(second_left, second_right, 1, 1)) + jitter
    inverse_one = inverse_factor(one_one)
    rows = dot(two_one, inverse_one, 1, 1, HIGHEST)
    remainder = two_two - dot(rows, rows, 1, 1, HIGHEST)
    cross = dot(rows, inverse_one, 1, 0, HIGHEST)
    inverse_two = inverse_factor(remainder)
    inverse[0:PIVOTS, 0:PIVOTS] = inverse_one
    inverse[0:PIVOTS, PIVOTS:] = jnp.zeros((PIVOTS, PIVOTS), F32)
    inverse[PIVOTS:, 0:PIVOTS] = -dot(inverse_two, cross, 1, 0, HIGHEST)
    inverse[PIVOTS:, PIVOTS:] = inverse_two

    pivots_left = jnp.concatenate([first_left, second_left], axis=0)
    pivots_right = jnp.concatenate([first_right, second_right], axis=0)
    weights_t = dot(coeffs_t[...], inverse[...], 1, 0, HIGHEST)

    def factor_step(i, carry):
        at_rows = pl.ds(pl.multiple_of(i * CHUNK, CHUNK), CHUNK)
        block = jnp.exp(dot(left[at_rows, :], pivots_right, 1, 1))
        factor[at_rows, :] = dot(block, inverse[...], 1, 1, HIGHEST)
        return carry

    lax.fori_loop(0, CHUNKS, factor_step, 0)

    def probes_of(c):
        columns = jnp.exp(dot(pivots_left, right[c]))
        return dot(weights_t, columns, 1, 0, HIGHEST)

    probes_t[...] = probes_of(6) + noise_t[...]
    probe_bf[6] = probes_t[...].astype(BF16)

    fill_tile(0, 4, 8)
    for k in (1, 2):
        near_p[k].wait_recv()
        fill_right(k)
        fill_tile(k, 0, 8)
    for one in far_n:
        one.wait_recv()
    relay_n = started([
        copy(far_noise.at[which[k]], near_noise.at[3 + k], SEM_RN + k, y_mates[k]) for k in range(3)
    ])
    for k in range(3):
        near_n[k].wait_recv()
        probe_bf[k] = (probes_of(k) + near_noise[k].astype(F32)).astype(BF16)
    for k in range(3):
        relay_p[k].wait_recv()
        fill_right(3 + k)
        fill_tile(3 + k, 0, 8)
    for k in range(3):
        relay_n[k].wait_recv()
        probe_bf[3 + k] = (probes_of(3 + k) + near_noise[3 + k].astype(F32)).astype(BF16)

    def out_step(i, carry):
        at_rows = pl.ds(pl.multiple_of(i * CHUNK, CHUNK), CHUNK)
        total = dot(tiles[0, at_rows, :], probe_bf[0], 1, 1)
        for c in range(1, 7):
            total = total + dot(tiles[c, at_rows, :], probe_bf[c], 1, 1)
        out_t[:, at_rows] = total.T * (1.0 / 32.0) + NOISE_WEIGHT * probes_t[:, at_rows]
        return carry

    lax.fori_loop(0, CHUNKS, out_step, 0)

    for group_of in (core_copy, far_p, near_p, x_copies, y_copies, z_copies, z_more, near_n, back, far_n, relay_p, relay_n):
        for one in group_of:
            one.wait_send()


def shards(points, pivots, owners, coeffs, noise):
    vmem, smem = pl.BlockSpec(memory_space=pltpu.VMEM), pl.BlockSpec(memory_space=pltpu.SMEM)
    block = (WIDTH, POINTS)
    out_t, factor = pl.pallas_call(
        kernel,
        out_shape=(
            jax.ShapeDtypeStruct(block, F32),
            jax.ShapeDtypeStruct((POINTS, RANK), F32),
        ),
        in_specs=[smem, vmem, vmem, vmem, vmem],
        out_specs=(vmem, vmem),
        scratch_shapes=[
            pltpu.VMEM(block, BF16),
            pltpu.VMEM((2, 64, LANES), BF16),
            pltpu.VMEM((64, LANES), BF16),
            pltpu.VMEM((4, 64, LANES), BF16),
            pltpu.VMEM((3, 64, LANES), BF16),
            pltpu.VMEM((3, 64, LANES), BF16),
            pltpu.VMEM((7, 64, LANES), BF16),
            pltpu.VMEM((2, 64, LANES), BF16),
            pltpu.VMEM((2,) + block, BF16),
            pltpu.VMEM((2,) + block, BF16),
            pltpu.VMEM((6,) + block, BF16),
            pltpu.VMEM((6,) + block, BF16),
            pltpu.VMEM((POINTS, LANES), BF16),
            pltpu.VMEM((7, LANES, POINTS), BF16),
            pltpu.VMEM((7, POINTS, POINTS), BF16),
            pltpu.VMEM((RANK, RANK), F32),
            pltpu.VMEM((7,) + block, BF16),
            pltpu.VMEM(block, F32),
            pltpu.SemaphoreType.DMA((SEMS,)),
            pltpu.SemaphoreType.DMA((SEMS,)),
        ],
        compiler_params=pltpu.CompilerParams(
            collective_id=0, has_side_effects=True, vmem_limit_bytes=60 * 1024 * 1024
        ),
    )(owners, pivots, points.T, coeffs.T, noise.T)
    return out_t.T, factor


def solution(mesh):
    in_specs = (P(("gx", "gy"), None), P(), P(), P(), P(("gx", "gy"), None))
    out_specs = (P(("gx", "gy"), None), P(("gx", "gy"), None))
    return jax.shard_map(shards, mesh=mesh, in_specs=in_specs, out_specs=out_specs, check_vma=False)
```

```python
import jax
import jax.numpy as jnp
from jax import lax
from jax.experimental import pallas as pl
from jax.experimental.pallas import tpu as pltpu
from jax.sharding import PartitionSpec as P

MESH = pl.DeviceIdType.MESH
F32, BF16 = jnp.float32, jnp.bfloat16
HIGHEST = lax.Precision.HIGHEST

POINTS = 1024
WIDTH = 64
PIVOTS = 128
RANK = 256
SCALE = 32.0
JITTER = 0.1
NOISE_WEIGHT = 0.5
LANES = 128
CHUNK = 128
CHUNKS = POINTS // CHUNK
TILE_ROWS = 512

FIRST_ROUND = (1, 15, 2, 14, 8)
SECOND_ROUND = (5, 11)

PLUS = ((1, 0), (3, 0), (0, 1), (0, 3))
COVER = ((2, 1), (1, 3), (3, 2))

SEM_CORE, SEM_PLUS, SEM_COVER, SEM_Z, SEM_CORE_BACK = 0, 1, 5, 8, 15
SEM_ZP, SEM_ZN, SEM_OP, SEM_ON, SEM_RP, SEM_RN = 16, 18, 20, 23, 26, 29
SEMS = 32
OUT_ROWS = 256


def dot(a, b, ca=1, cb=0, precision=None):
    return lax.dot_general(
        a, b, (((ca,), (cb,)), ((), ())), precision=precision, preferred_element_type=F32
    )


def three_parts(value):
    high = value.astype(BF16).astype(F32)
    rest = value - high
    middle = rest.astype(BF16).astype(F32)
    return high, middle, rest - middle


def right_columns(points_t):
    count = points_t.shape[1]
    norm = jnp.sum(points_t * points_t, axis=0, keepdims=True) * (-1.0 / SCALE)
    high, middle, low = three_parts(norm)
    row = lax.broadcasted_iota(jnp.int32, (LANES - WIDTH, count), 0)
    extra = jnp.where(row == 0, high, 0.0)
    extra = jnp.where(row == 1, middle, extra)
    extra = jnp.where(row == 2, low, extra)
    extra = jnp.where((row >= 3) & (row < 6), 1.0, extra)
    return extra


def left_columns(points_t):
    count = points_t.shape[1]
    norm = jnp.sum(points_t * points_t, axis=0, keepdims=True) * (-1.0 / SCALE)
    high, middle, low = three_parts(norm)
    row = lax.broadcasted_iota(jnp.int32, (LANES - WIDTH, count), 0)
    extra = jnp.where(row < 3, 1.0, 0.0)
    extra = jnp.where(row == 3, high, extra)
    extra = jnp.where(row == 4, middle, extra)
    extra = jnp.where(row == 5, low, extra)
    return extra


def pivot_rows(value):
    norm = jnp.sum(value * value, axis=1, keepdims=True) * (-1.0 / SCALE)
    high, middle, low = three_parts(norm)
    lane = lax.broadcasted_iota(jnp.int32, value.shape, 1)
    left = value * (2.0 / SCALE)
    left = jnp.where((lane >= 64) & (lane < 67), 1.0, left)
    left = jnp.where(lane == 67, high, left)
    left = jnp.where(lane == 68, middle, left)
    left = jnp.where(lane == 69, low, left)
    right = jnp.where(lane == 64, high, value)
    right = jnp.where(lane == 65, middle, right)
    right = jnp.where(lane == 66, low, right)
    right = jnp.where((lane >= 67) & (lane < 70), 1.0, right)
    return left.astype(BF16), right.astype(BF16)


def reciprocal(value):
    guess = pl.reciprocal(value, approx=True)
    guess = guess * (2.0 - value * guess)
    return guess * (2.0 - value * guess)


def inverse_factor(matrix):
    n = PIVOTS
    count = n // 8
    tiles = [matrix[8 * t : 8 * t + 8, :] for t in range(count)]
    lane = lax.broadcasted_iota(jnp.int32, (8, n), 1)
    sub = lax.broadcasted_iota(jnp.int32, (8, n), 0)
    full = (8, n)
    out = []
    for b in range(count):
        base = 8 * b
        inside = (lane >= base) & (lane < base + 8)
        columns = [jnp.broadcast_to(tiles[b][:, base + j : base + j + 1], full) for j in range(8)]
        s = {
            (i, j): jnp.broadcast_to(columns[j][i : i + 1, :], full)
            for j in range(8)
            for i in range(j, 8)
        }
        panel = jnp.where(inside, jnp.where(lane == sub + base, 1.0, 0.0), tiles[b])
        w = [jnp.broadcast_to(panel[i : i + 1, :], full) for i in range(8)]
        z, m = [None] * 8, {}
        for p in range(0, 8, 2):
            q = p + 1
            a, o, c = s[p, p], s[q, p], s[q, q]
            inv = reciprocal(a * c - o * o)
            for i in range(p + 2, 8):
                m[i, p] = (s[i, p] * c - s[i, q] * o) * inv
                m[i, q] = (s[i, q] * a - s[i, p] * o) * inv
            for i in range(p + 2, 8):
                for j in range(p + 2, i + 1):
                    s[i, j] = s[i, j] - (m[i, p] * s[j, p] + m[i, q] * s[j, q])
            z[p] = (w[p] * c - w[q] * o) * inv
            z[q] = (w[q] * a - w[p] * o) * inv
            for i in range(p + 2, 8):
                w[i] = w[i] - (m[i, p] * w[p] + m[i, q] * w[q])
            ratio = 1.0 / a
            s["first", p] = w[p] * lax.rsqrt(a)
            s["second", p] = (w[q] - o * ratio * w[p]) * lax.rsqrt(c - o * ratio * o)
        for p in (4, 2, 0):
            for j in (p, p + 1):
                for i in range(p + 2, 8):
                    z[j] = z[j] - m[i, j] * z[i]
        for t in range(b + 1, count):
            now = jnp.where(inside, 0.0, tiles[t])
            parts = [
                jnp.broadcast_to(tiles[t][:, base + j : base + j + 1], full) * z[j] for j in range(8)
            ]
            while len(parts) > 1:
                parts = [parts[i] + parts[i + 1] for i in range(0, len(parts), 2)]
            tiles[t] = now - parts[0]
        done = s["first", 0]
        for i in range(1, 8):
            done = jnp.where(sub == i, s["first" if i % 2 == 0 else "second", i - i % 2], done)
        out.append(jnp.where(lane < base + 8, done, 0.0))
    return jnp.concatenate(out, axis=0)


def kernel(
    owners, pivots, points_hbm, coeffs_hbm, noise_hbm, out_hbm, left_hbm, right_hbm, inverse_hbm,
    out_t, left, pivots_right, inverse, points_t, coeffs_t, noise_t, noise_bf, mine, core_buf, stage, plus_buf, cover_buf, z_buf, pivot_buf, far_points, far_noise,
    near_points, near_noise, right, tiles, probe_bf, probes_t, totals, send, recv, loaded, saved,
):
    loads = [
        pltpu.make_async_copy(source, target, loaded.at[i])
        for i, (source, target) in enumerate(
            ((points_hbm, points_t), (noise_hbm, noise_t), (coeffs_hbm, coeffs_t))
        )
    ]
    for load in loads:
        load.start()
    gx, gy = lax.axis_index("gx"), lax.axis_index("gy")
    core, z_lo, x = gx % 2, (gx // 2) % 4, gx // 8
    z_hi, y = gy // 4, gy % 4
    z = z_hi * 4 + z_lo
    group = gx * 4 + z_hi
    me = gx * 16 + gy

    def at(x, z, core, y):
        return (((x % 4) * 4 + z % 4) * 2 + core, (z // 4) * 4 + y % 4)

    def group_at(step):
        other = (group + step + 128) % 128
        return (other // 4, (other % 4) * 4 + y)

    other_core = at(x, z, 1 - core, y)
    y_mates = [at(x, z, core, y + k) for k in (1, 2, 3)]
    plus_mates = [at(x + i, z, core, y + j) for i, j in PLUS]
    cover_mates = [at(x + i, z, core, y + j) for i, j in COVER]
    cover_sources = [at(x + 4 - i, z, core, y + 4 - j) for i, j in COVER]
    z_mates = [at(x, (z + d) % 16, core, y) for d in FIRST_ROUND + SECOND_ROUND]
    after, before = group_at(1), group_at(-1)

    barrier = pltpu.get_barrier_semaphore()
    peers = [other_core] + plus_mates[0:2] + y_mates + cover_sources + z_mates + [after, before]
    for peer in peers:
        pl.semaphore_signal(barrier, inc=1, device_id=peer, device_id_type=MESH)

    def copy(source, target, number, device):
        return pltpu.make_async_remote_copy(
            src_ref=source, dst_ref=target, send_sem=send.at[number], recv_sem=recv.at[number],
            device_id=device, device_id_type=MESH,
        )

    def started(copies):
        for one in copies:
            one.start()
        return copies

    def arrived(copies):
        for one in copies:
            one.wait_recv()

    def either(a, b):
        return jnp.where(a == 0, b, a)

    def fill_tile(c, low=0, high=POINTS // TILE_ROWS):
        def step(i, carry):
            at_rows = pl.ds(pl.multiple_of(i * TILE_ROWS, TILE_ROWS), TILE_ROWS)
            tiles[c, at_rows, :] = jnp.exp(dot(left[at_rows, :], right[c])).astype(BF16)
            return carry

        lax.fori_loop(low, high, step, 0)

    def fill_right(c):
        block = near_points[c].astype(F32)
        right[c, 0:WIDTH, :] = near_points[c]
        right[c, WIDTH:, :] = right_columns(block).astype(BF16)

    loads[0].wait()
    index = lax.broadcasted_iota(jnp.int32, (PIVOTS, POINTS), 1)
    for turn in range(2):
        wanted = jnp.where(owners[turn] == me, pivots[turn : turn + 1, :], -1)
        wanted = jnp.broadcast_to(wanted, (PIVOTS, PIVOTS)).T[:, 0:1]
        chosen = jnp.where(index == wanted, 1.0, 0.0).astype(BF16)
        rows = dot(chosen, points_t[...], 1, 1).astype(BF16)
        for half in range(2):
            mine[half, :, WIDTH * turn : WIDTH * (turn + 1)] = rows[64 * half : 64 * half + 64, :]

    pl.semaphore_wait(barrier, len(peers))

    def save(source, target, number):
        one = pltpu.make_async_copy(source, target, saved.at[number])
        one.start()
        return one

    core_copy = started([copy(mine.at[1 - core], core_buf, SEM_CORE, other_core)])
    near_p = started([copy(points_t, near_points.at[k], SEM_OP + k, y_mates[k]) for k in range(3)])

    own = points_t[...].astype(F32)
    right[6, 0:WIDTH, :] = points_t[...]
    right[6, WIDTH:, :] = right_columns(own).astype(BF16)
    left[...] = jnp.concatenate([own * (2.0 / SCALE), left_columns(own)], axis=0).T.astype(BF16)
    saves = [save(left, left_hbm, 0)]
    loads[1].wait()
    noise_bf[...] = noise_t[...].astype(BF16)
    loads[2].wait()

    arrived(core_copy)
    stage[0] = mine[core] + core_buf[...]

    rounds = len(FIRST_ROUND)
    z_first = started([copy(stage.at[0], z_buf.at[k], SEM_Z + k, z_mates[k]) for k in range(rounds)])
    fill_tile(6, 0, 1)
    arrived(z_first[0:4])
    gathered = stage[0]
    for k in range(4):
        gathered = either(gathered, z_buf[k])
    stage[1] = gathered
    z_second = started([
        copy(stage.at[1], z_buf.at[rounds + k], SEM_Z + rounds + k, z_mates[rounds + k])
        for k in range(len(SECOND_ROUND))
    ])
    fill_tile(6, 1, 2)
    arrived(z_first[4:])
    arrived(z_second)
    gathered = stage[1]
    for k in range(4, 7):
        gathered = either(gathered, z_buf[k])
    stage[2] = gathered
    plus = started([copy(stage.at[2], plus_buf.at[k], SEM_PLUS + k, plus_mates[k]) for k in range(4)])
    far_p = started([
        copy(points_t, far_points.at[0], SEM_ZP, after),
        copy(points_t, far_points.at[1], SEM_ZP + 1, before),
    ])
    arrived(near_p[2:])
    fill_right(2)
    fill_tile(2, 0, 1)
    arrived(plus)
    gathered = stage[2]
    for k in range(4):
        gathered = either(gathered, plus_buf[k])
    stage[3] = gathered
    cover = started([copy(stage.at[3], cover_buf.at[k], SEM_COVER + k, cover_mates[k]) for k in range(3)])
    fill_tile(2, 1, 2)
    arrived(near_p[0:1])
    fill_right(0)
    fill_tile(0)
    arrived(cover)
    gathered = stage[3]
    for k in range(3):
        gathered = either(gathered, cover_buf[k])
    pivot_buf[core] = gathered
    back = started([copy(pivot_buf.at[core], pivot_buf.at[core], SEM_CORE_BACK, other_core)])
    near_n = started([copy(noise_bf, near_noise.at[k], SEM_ON + k, y_mates[k]) for k in range(3)])
    far_n = started([
        copy(noise_bf, far_noise.at[0], SEM_ZN, after),
        copy(noise_bf, far_noise.at[1], SEM_ZN + 1, before),
    ])
    arrived(near_p[1:2])
    fill_right(1)
    fill_tile(1)
    arrived(back)

    both = jnp.concatenate([pivot_buf[0], pivot_buf[1]], axis=0).astype(F32)
    lane = lax.broadcasted_iota(jnp.int32, both.shape, 1)
    first = jnp.where(lane < WIDTH, both, 0.0)
    second = jnp.where(lane < WIDTH, pltpu.roll(both, WIDTH, 1), 0.0)
    first_left, first_right = pivot_rows(first)
    second_left, second_right = pivot_rows(second)
    square = lax.broadcasted_iota(jnp.int32, (PIVOTS, PIVOTS), 0) == lax.broadcasted_iota(
        jnp.int32, (PIVOTS, PIVOTS), 1
    )
    jitter = jnp.where(square, JITTER, 0.0)
    one_one = jnp.exp(dot(first_left, first_right, 1, 1)) + jitter
    two_one = jnp.exp(dot(second_left, first_right, 1, 1))
    two_two = jnp.exp(dot(second_left, second_right, 1, 1)) + jitter
    inverse_one = inverse_factor(one_one)
    inverse[0:PIVOTS, 0:PIVOTS] = inverse_one

    arrived(far_p)
    which = [1 - (y + k) // 4 for k in (1, 2, 3)]
    relay_p = started([
        copy(far_points.at[which[k]], near_points.at[3 + k], SEM_RP + k, y_mates[k]) for k in range(3)
    ])

    rows = dot(two_one, inverse_one, 1, 1, HIGHEST)
    remainder = two_two - dot(rows, rows, 1, 1, HIGHEST)
    cross = dot(rows, inverse_one, 1, 0, HIGHEST)
    inverse_two = inverse_factor(remainder)
    inverse[0:PIVOTS, PIVOTS:] = jnp.zeros((PIVOTS, PIVOTS), F32)
    inverse[PIVOTS:, 0:PIVOTS] = -dot(inverse_two, cross, 1, 0, HIGHEST)
    inverse[PIVOTS:, PIVOTS:] = inverse_two
    saves.append(save(inverse, inverse_hbm, 1))
    pivots_right[...] = jnp.concatenate([first_right, second_right], axis=0)
    saves.append(save(pivots_right, right_hbm, 2))
    pivots_left = jnp.concatenate([first_left, second_left], axis=0)
    weights_t = dot(coeffs_t[...], inverse[...], 1, 0, HIGHEST)
    weights = jnp.concatenate(three_parts(weights_t), axis=0).astype(BF16)

    def probes_of(c):
        high, middle, low = three_parts(jnp.exp(dot(pivots_left, right[c])))
        one = dot(weights, high.astype(BF16))
        two = dot(weights[0 : 2 * WIDTH], middle.astype(BF16))
        three = dot(weights[0:WIDTH], low.astype(BF16))
        small = one[2 * WIDTH :] + two[WIDTH:] + three
        return one[0:WIDTH] + ((one[WIDTH : 2 * WIDTH] + two[0:WIDTH]) + small)

    probes_t[...] = probes_of(6) + noise_t[...]
    probe_bf[6] = probes_t[...].astype(BF16)
    for k in range(3):
        arrived(near_n[k : k + 1])
        probe_bf[k] = (probes_of(k) + near_noise[k].astype(F32)).astype(BF16)

    arrived(far_n)
    relay_n = started([
        copy(far_noise.at[which[k]], near_noise.at[3 + k], SEM_RN + k, y_mates[k]) for k in range(3)
    ])

    def near_step(i, carry):
        at_rows = pl.ds(pl.multiple_of(i * OUT_ROWS, OUT_ROWS), OUT_ROWS)
        total = dot(tiles[6, at_rows, :], probe_bf[6], 1, 1)
        for c in range(3):
            total = total + dot(tiles[c, at_rows, :], probe_bf[c], 1, 1)
        totals[at_rows, :] = total
        return carry

    lax.fori_loop(0, POINTS // OUT_ROWS, near_step, 0)

    for k in (2, 0, 1):
        arrived(relay_p[k : k + 1])
        fill_right(3 + k)
        fill_tile(3 + k)
    for k in (2, 0, 1):
        arrived(relay_n[k : k + 1])
        probe_bf[3 + k] = (probes_of(3 + k) + near_noise[3 + k].astype(F32)).astype(BF16)

    def far_step(i, carry):
        at_rows = pl.ds(pl.multiple_of(i * OUT_ROWS, OUT_ROWS), OUT_ROWS)
        total = totals[at_rows, :]
        for c in range(3, 6):
            total = total + dot(tiles[c, at_rows, :], probe_bf[c], 1, 1)
        out_t[:, at_rows] = total.T * (1.0 / 32.0) + NOISE_WEIGHT * probes_t[:, at_rows]
        return carry

    lax.fori_loop(0, POINTS // OUT_ROWS, far_step, 0)
    saves.append(save(out_t, out_hbm, 3))

    for copies in (
        core_copy, near_p, z_first, z_second, plus, far_p, cover, back, near_n, far_n, relay_p, relay_n
    ):
        for one in copies:
            one.wait_send()
    for one in saves:
        one.wait()


def factor_kernel(left, pivots_right, inverse, given_t, factor, out_t):
    block = jnp.exp(dot(left[...], pivots_right[...], 1, 1))
    factor[...] = dot(block, inverse[...], 1, 1, HIGHEST)
    out_t[...] = given_t[...]


def shards(points, pivots, owners, coeffs, noise):
    vmem, smem = pl.BlockSpec(memory_space=pltpu.VMEM), pl.BlockSpec(memory_space=pltpu.SMEM)
    anywhere = pl.BlockSpec(memory_space=pl.ANY)
    block = (WIDTH, POINTS)
    part = (64, LANES)
    given_t, left, pivots_right, inverse = pl.pallas_call(
        kernel,
        out_shape=(
            jax.ShapeDtypeStruct(block, F32),
            jax.ShapeDtypeStruct((POINTS, LANES), BF16),
            jax.ShapeDtypeStruct((RANK, LANES), BF16),
            jax.ShapeDtypeStruct((RANK, RANK), F32),
        ),
        in_specs=[smem, vmem, anywhere, anywhere, anywhere],
        out_specs=(anywhere, anywhere, anywhere, anywhere),
        scratch_shapes=[
            pltpu.VMEM(block, F32),
            pltpu.VMEM((POINTS, LANES), BF16),
            pltpu.VMEM((RANK, LANES), BF16),
            pltpu.VMEM((RANK, RANK), F32),
            pltpu.VMEM(block, BF16),
            pltpu.VMEM((WIDTH, RANK), F32),
            pltpu.VMEM(block, F32),
            pltpu.VMEM(block, BF16),
            pltpu.VMEM((2,) + part, BF16),
            pltpu.VMEM(part, BF16),
            pltpu.VMEM((4,) + part, BF16),
            pltpu.VMEM((4,) + part, BF16),
            pltpu.VMEM((3,) + part, BF16),
            pltpu.VMEM((7,) + part, BF16),
            pltpu.VMEM((2,) + part, BF16),
            pltpu.VMEM((2,) + block, BF16),
            pltpu.VMEM((2,) + block, BF16),
            pltpu.VMEM((6,) + block, BF16),
            pltpu.VMEM((6,) + block, BF16),
            pltpu.VMEM((7, LANES, POINTS), BF16),
            pltpu.VMEM((7, POINTS, POINTS), BF16),
            pltpu.VMEM((7,) + block, BF16),
            pltpu.VMEM(block, F32),
            pltpu.VMEM((POINTS, WIDTH), F32),
            pltpu.SemaphoreType.DMA((SEMS,)),
            pltpu.SemaphoreType.DMA((SEMS,)),
            pltpu.SemaphoreType.DMA((3,)),
            pltpu.SemaphoreType.DMA((4,)),
        ],
        compiler_params=pltpu.CompilerParams(
            collective_id=0, has_side_effects=True, vmem_limit_bytes=62 * 1024 * 1024
        ),
    )(owners, pivots, points.T, coeffs.T, noise.T)
    steps = 4
    tall = POINTS // steps
    factor, out_t = pl.pallas_call(
        factor_kernel,
        grid=(steps,),
        out_shape=(
            jax.ShapeDtypeStruct((POINTS, RANK), F32),
            jax.ShapeDtypeStruct(block, F32),
        ),
        in_specs=[
            pl.BlockSpec((tall, LANES), lambda i: (i, 0)),
            pl.BlockSpec((RANK, LANES), lambda i: (0, 0)),
            pl.BlockSpec((RANK, RANK), lambda i: (0, 0)),
            pl.BlockSpec((WIDTH, tall), lambda i: (0, i)),
        ],
        out_specs=(
            pl.BlockSpec((tall, RANK), lambda i: (i, 0)),
            pl.BlockSpec((WIDTH, tall), lambda i: (0, i)),
        ),
        compiler_params=pltpu.CompilerParams(vmem_limit_bytes=62 * 1024 * 1024),
    )(left, pivots_right, inverse, given_t)
    return out_t.T, factor


def solution(mesh):
    in_specs = (P(("gx", "gy"), None), P(), P(), P(), P(("gx", "gy"), None))
    out_specs = (P(("gx", "gy"), None), P(("gx", "gy"), None))
    return jax.shard_map(shards, mesh=mesh, in_specs=in_specs, out_specs=out_specs, check_vma=False)
```

```python
import jax
import jax.numpy as jnp
from jax import lax
from jax.experimental import pallas as pl
from jax.experimental.pallas import tpu as pltpu
from jax.sharding import PartitionSpec as P

MESH = pl.DeviceIdType.MESH
F32, BF16 = jnp.float32, jnp.bfloat16
HIGHEST = lax.Precision.HIGHEST

POINTS = 1024
WIDTH = 64
PIVOTS = 128
RANK = 256
SCALE = 32.0
JITTER = 0.1
NOISE_WEIGHT = 0.5
LANES = 128
CHUNK = 128
CHUNKS = POINTS // CHUNK
TILE_ROWS = 512

FIRST_ROUND = (1, 15, 2, 14, 8)
SECOND_ROUND = (5, 11)

PLUS = ((1, 0), (3, 0), (0, 1), (0, 3))
COVER = ((2, 1), (1, 3), (3, 2))

SEM_CORE, SEM_PLUS, SEM_COVER, SEM_Z, SEM_CORE_BACK = 0, 1, 5, 8, 15
SEM_ZP, SEM_ZN, SEM_OP, SEM_ON, SEM_RP, SEM_RN = 16, 18, 20, 23, 26, 29
SEM_PASS = 32
SEMS = 33
OUT_ROWS = 256


def dot(a, b, ca=1, cb=0, precision=None):
    return lax.dot_general(
        a, b, (((ca,), (cb,)), ((), ())), precision=precision, preferred_element_type=F32
    )


def three_parts(value):
    high = value.astype(BF16).astype(F32)
    rest = value - high
    middle = rest.astype(BF16).astype(F32)
    return high, middle, rest - middle


def right_columns(points_t):
    count = points_t.shape[1]
    norm = jnp.sum(points_t * points_t, axis=0, keepdims=True) * (-1.0 / SCALE)
    high, middle, low = three_parts(norm)
    row = lax.broadcasted_iota(jnp.int32, (LANES - WIDTH, count), 0)
    extra = jnp.where(row == 0, high, 0.0)
    extra = jnp.where(row == 1, middle, extra)
    extra = jnp.where(row == 2, low, extra)
    extra = jnp.where((row >= 3) & (row < 6), 1.0, extra)
    return extra


def left_columns(points_t):
    count = points_t.shape[1]
    norm = jnp.sum(points_t * points_t, axis=0, keepdims=True) * (-1.0 / SCALE)
    high, middle, low = three_parts(norm)
    row = lax.broadcasted_iota(jnp.int32, (LANES - WIDTH, count), 0)
    extra = jnp.where(row < 3, 1.0, 0.0)
    extra = jnp.where(row == 3, high, extra)
    extra = jnp.where(row == 4, middle, extra)
    extra = jnp.where(row == 5, low, extra)
    return extra


def pivot_rows(value):
    norm = jnp.sum(value * value, axis=1, keepdims=True) * (-1.0 / SCALE)
    high, middle, low = three_parts(norm)
    lane = lax.broadcasted_iota(jnp.int32, value.shape, 1)
    left = value * (2.0 / SCALE)
    left = jnp.where((lane >= 64) & (lane < 67), 1.0, left)
    left = jnp.where(lane == 67, high, left)
    left = jnp.where(lane == 68, middle, left)
    left = jnp.where(lane == 69, low, left)
    right = jnp.where(lane == 64, high, value)
    right = jnp.where(lane == 65, middle, right)
    right = jnp.where(lane == 66, low, right)
    right = jnp.where((lane >= 67) & (lane < 70), 1.0, right)
    return left.astype(BF16), right.astype(BF16)


def reciprocal(value):
    guess = pl.reciprocal(value, approx=True)
    guess = guess * (2.0 - value * guess)
    return guess * (2.0 - value * guess)


def inverse_factor(matrix):
    n = PIVOTS
    count = n // 8
    tiles = [matrix[8 * t : 8 * t + 8, :] for t in range(count)]
    lane = lax.broadcasted_iota(jnp.int32, (8, n), 1)
    sub = lax.broadcasted_iota(jnp.int32, (8, n), 0)
    full = (8, n)
    out = []
    for b in range(count):
        base = 8 * b
        inside = (lane >= base) & (lane < base + 8)
        columns = [jnp.broadcast_to(tiles[b][:, base + j : base + j + 1], full) for j in range(8)]
        s = {
            (i, j): jnp.broadcast_to(columns[j][i : i + 1, :], full)
            for j in range(8)
            for i in range(j, 8)
        }
        panel = jnp.where(inside, jnp.where(lane == sub + base, 1.0, 0.0), tiles[b])
        w = [jnp.broadcast_to(panel[i : i + 1, :], full) for i in range(8)]
        z, m = [None] * 8, {}
        for p in range(0, 8, 2):
            q = p + 1
            a, o, c = s[p, p], s[q, p], s[q, q]
            inv = reciprocal(a * c - o * o)
            for i in range(p + 2, 8):
                m[i, p] = (s[i, p] * c - s[i, q] * o) * inv
                m[i, q] = (s[i, q] * a - s[i, p] * o) * inv
            for i in range(p + 2, 8):
                for j in range(p + 2, i + 1):
                    s[i, j] = s[i, j] - (m[i, p] * s[j, p] + m[i, q] * s[j, q])
            z[p] = (w[p] * c - w[q] * o) * inv
            z[q] = (w[q] * a - w[p] * o) * inv
            for i in range(p + 2, 8):
                w[i] = w[i] - (m[i, p] * w[p] + m[i, q] * w[q])
            ratio = 1.0 / a
            s["first", p] = w[p] * lax.rsqrt(a)
            s["second", p] = (w[q] - o * ratio * w[p]) * lax.rsqrt(c - o * ratio * o)
        for p in (4, 2, 0):
            for j in (p, p + 1):
                for i in range(p + 2, 8):
                    z[j] = z[j] - m[i, j] * z[i]
        for t in range(b + 1, count):
            now = jnp.where(inside, 0.0, tiles[t])
            parts = [
                jnp.broadcast_to(tiles[t][:, base + j : base + j + 1], full) * z[j] for j in range(8)
            ]
            while len(parts) > 1:
                parts = [parts[i] + parts[i + 1] for i in range(0, len(parts), 2)]
            tiles[t] = now - parts[0]
        done = s["first", 0]
        for i in range(1, 8):
            done = jnp.where(sub == i, s["first" if i % 2 == 0 else "second", i - i % 2], done)
        out.append(jnp.where(lane < base + 8, done, 0.0))
    return jnp.concatenate(out, axis=0)


def kernel(
    owners, pivots, points_hbm, coeffs_hbm, noise_hbm, out_hbm, left_hbm, right_hbm, inverse_hbm,
    out_t, left, pivots_right, inverse, points_t, coeffs_t, noise_t, noise_bf, mine, core_buf, stage, plus_buf, cover_buf, z_buf, pivot_buf, far_points, far_noise,
    near_points, near_noise, right, tiles, probe_bf, probes_t, totals, far_probes, send, recv, loaded, saved,
):
    loads = [
        pltpu.make_async_copy(source, target, loaded.at[i])
        for i, (source, target) in enumerate(
            ((points_hbm, points_t), (noise_hbm, noise_t), (coeffs_hbm, coeffs_t))
        )
    ]
    for load in loads:
        load.start()
    gx, gy = lax.axis_index("gx"), lax.axis_index("gy")
    core, z_lo, x = gx % 2, (gx // 2) % 4, gx // 8
    z_hi, y = gy // 4, gy % 4
    z = z_hi * 4 + z_lo
    group = gx * 4 + z_hi
    me = gx * 16 + gy

    def at(x, z, core, y):
        return (((x % 4) * 4 + z % 4) * 2 + core, (z // 4) * 4 + y % 4)

    def group_at(step):
        other = (group + step + 128) % 128
        return (other // 4, (other % 4) * 4 + y)

    other_core = at(x, z, 1 - core, y)
    y_mates = [at(x, z, core, y + k) for k in (1, 2, 3)]
    plus_mates = [at(x + i, z, core, y + j) for i, j in PLUS]
    cover_mates = [at(x + i, z, core, y + j) for i, j in COVER]
    cover_sources = [at(x + 4 - i, z, core, y + 4 - j) for i, j in COVER]
    z_mates = [at(x, (z + d) % 16, core, y) for d in FIRST_ROUND + SECOND_ROUND]
    after, before = group_at(1), group_at(-1)

    barrier = pltpu.get_barrier_semaphore()
    peers = [other_core] + plus_mates[0:2] + y_mates + cover_sources + z_mates + [after, before]
    for peer in peers:
        pl.semaphore_signal(barrier, inc=1, device_id=peer, device_id_type=MESH)

    def copy(source, target, number, device):
        return pltpu.make_async_remote_copy(
            src_ref=source, dst_ref=target, send_sem=send.at[number], recv_sem=recv.at[number],
            device_id=device, device_id_type=MESH,
        )

    def started(copies):
        for one in copies:
            one.start()
        return copies

    def arrived(copies):
        for one in copies:
            one.wait_recv()

    def either(a, b):
        return jnp.where(a == 0, b, a)

    def fill_tile(c, low=0, high=POINTS // TILE_ROWS):
        def step(i, carry):
            at_rows = pl.ds(pl.multiple_of(i * TILE_ROWS, TILE_ROWS), TILE_ROWS)
            tiles[c, at_rows, :] = jnp.exp(dot(left[at_rows, :], right[c])).astype(BF16)
            return carry

        lax.fori_loop(low, high, step, 0)

    def fill_right(c):
        block = near_points[c].astype(F32)
        right[c, 0:WIDTH, :] = near_points[c]
        right[c, WIDTH:, :] = right_columns(block).astype(BF16)

    loads[0].wait()
    index = lax.broadcasted_iota(jnp.int32, (PIVOTS, POINTS), 1)
    for turn in range(2):
        wanted = jnp.where(owners[turn] == me, pivots[turn : turn + 1, :], -1)
        wanted = jnp.broadcast_to(wanted, (PIVOTS, PIVOTS)).T[:, 0:1]
        chosen = jnp.where(index == wanted, 1.0, 0.0).astype(BF16)
        rows = dot(chosen, points_t[...], 1, 1).astype(BF16)
        for half in range(2):
            mine[half, :, WIDTH * turn : WIDTH * (turn + 1)] = rows[64 * half : 64 * half + 64, :]

    pl.semaphore_wait(barrier, len(peers))

    def save(source, target, number):
        one = pltpu.make_async_copy(source, target, saved.at[number])
        one.start()
        return one

    core_copy = started([copy(mine.at[1 - core], core_buf, SEM_CORE, other_core)])
    near_p = started([copy(points_t, near_points.at[k], SEM_OP + k, y_mates[k]) for k in range(3)])

    own = points_t[...].astype(F32)
    right[6, 0:WIDTH, :] = points_t[...]
    right[6, WIDTH:, :] = right_columns(own).astype(BF16)
    left[...] = jnp.concatenate([own * (2.0 / SCALE), left_columns(own)], axis=0).T.astype(BF16)
    saves = [save(left, left_hbm, 0)]
    loads[1].wait()
    noise_bf[...] = noise_t[...].astype(BF16)
    loads[2].wait()

    arrived(core_copy)
    stage[0] = mine[core] + core_buf[...]

    rounds = len(FIRST_ROUND)
    z_first = started([copy(stage.at[0], z_buf.at[k], SEM_Z + k, z_mates[k]) for k in range(rounds)])
    fill_tile(6, 0, 1)
    arrived(z_first[0:4])
    gathered = stage[0]
    for k in range(4):
        gathered = either(gathered, z_buf[k])
    stage[1] = gathered
    z_second = started([
        copy(stage.at[1], z_buf.at[rounds + k], SEM_Z + rounds + k, z_mates[rounds + k])
        for k in range(len(SECOND_ROUND))
    ])
    far_p = started([
        copy(points_t, far_points.at[0], SEM_ZP, after),
        copy(points_t, far_points.at[1], SEM_ZP + 1, before),
    ])
    fill_tile(6, 1, 2)
    arrived(z_first[4:])
    arrived(z_second)
    gathered = stage[1]
    for k in range(4, 7):
        gathered = either(gathered, z_buf[k])
    stage[2] = gathered
    plus = started([copy(stage.at[2], plus_buf.at[k], SEM_PLUS + k, plus_mates[k]) for k in range(4)])
    arrived(near_p[2:])
    fill_right(2)
    fill_tile(2, 0, 1)
    arrived(plus)
    gathered = stage[2]
    for k in range(4):
        gathered = either(gathered, plus_buf[k])
    stage[3] = gathered
    cover = started([copy(stage.at[3], cover_buf.at[k], SEM_COVER + k, cover_mates[k]) for k in range(3)])
    fill_tile(2, 1, 2)
    arrived(near_p[0:1])
    fill_right(0)
    fill_tile(0)
    arrived(cover)
    gathered = stage[3]
    for k in range(3):
        gathered = either(gathered, cover_buf[k])
    pivot_buf[core] = gathered
    back = started([copy(pivot_buf.at[core], pivot_buf.at[core], SEM_CORE_BACK, other_core)])
    near_n = started([copy(noise_bf, near_noise.at[k], SEM_ON + k, y_mates[k]) for k in (0, 2)])
    far_n = started([
        copy(noise_bf, far_noise.at[0], SEM_ZN, after),
        copy(noise_bf, far_noise.at[1], SEM_ZN + 1, before),
    ])
    arrived(near_p[1:2])
    fill_right(1)
    fill_tile(1)
    arrived(back)

    both = jnp.concatenate([pivot_buf[0], pivot_buf[1]], axis=0).astype(F32)
    lane = lax.broadcasted_iota(jnp.int32, both.shape, 1)
    first = jnp.where(lane < WIDTH, both, 0.0)
    second = jnp.where(lane < WIDTH, pltpu.roll(both, WIDTH, 1), 0.0)
    first_left, first_right = pivot_rows(first)
    second_left, second_right = pivot_rows(second)
    square = lax.broadcasted_iota(jnp.int32, (PIVOTS, PIVOTS), 0) == lax.broadcasted_iota(
        jnp.int32, (PIVOTS, PIVOTS), 1
    )
    jitter = jnp.where(square, JITTER, 0.0)
    one_one = jnp.exp(dot(first_left, first_right, 1, 1)) + jitter
    two_one = jnp.exp(dot(second_left, first_right, 1, 1))
    two_two = jnp.exp(dot(second_left, second_right, 1, 1)) + jitter
    inverse_one = inverse_factor(one_one)
    inverse[0:PIVOTS, 0:PIVOTS] = inverse_one

    arrived(near_n)
    upper, lower = pl.ds(0, WIDTH // 2), pl.ds(WIDTH // 2, WIDTH // 2)
    passed = started([
        copy(near_noise.at[0, upper], near_noise.at[1, upper], SEM_ON + 1, y_mates[0]),
        copy(near_noise.at[2, lower], near_noise.at[1, lower], SEM_PASS, y_mates[2]),
    ])
    arrived(far_p)
    which = [1 - (y + k) // 4 for k in (1, 2, 3)]
    relay_p = started([
        copy(far_points.at[which[k]], near_points.at[3 + k], SEM_RP + k, y_mates[k]) for k in range(3)
    ])

    rows = dot(two_one, inverse_one, 1, 1, HIGHEST)
    remainder = two_two - dot(rows, rows, 1, 1, HIGHEST)
    cross = dot(rows, inverse_one, 1, 0, HIGHEST)
    inverse_two = inverse_factor(remainder)
    inverse[0:PIVOTS, PIVOTS:] = jnp.zeros((PIVOTS, PIVOTS), F32)
    inverse[PIVOTS:, 0:PIVOTS] = -dot(inverse_two, cross, 1, 0, HIGHEST)
    inverse[PIVOTS:, PIVOTS:] = inverse_two
    saves.append(save(inverse, inverse_hbm, 1))
    pivots_right[...] = jnp.concatenate([first_right, second_right], axis=0)
    saves.append(save(pivots_right, right_hbm, 2))
    pivots_left = jnp.concatenate([first_left, second_left], axis=0)
    weights_t = dot(coeffs_t[...], inverse[...], 1, 0, HIGHEST)
    weights = jnp.concatenate(three_parts(weights_t), axis=0).astype(BF16)

    def probes_of(c):
        high, middle, low = three_parts(jnp.exp(dot(pivots_left, right[c])))
        one = dot(weights, high.astype(BF16))
        two = dot(weights[0 : 2 * WIDTH], middle.astype(BF16))
        three = dot(weights[0:WIDTH], low.astype(BF16))
        small = one[2 * WIDTH :] + two[WIDTH:] + three
        return one[0:WIDTH] + ((one[WIDTH : 2 * WIDTH] + two[0:WIDTH]) + small)

    probes_t[...] = probes_of(6) + noise_t[...]
    probe_bf[6] = probes_t[...].astype(BF16)
    for k in (0, 2, 1):
        if k == 1:
            arrived(passed)
        probe_bf[k] = (probes_of(k) + near_noise[k].astype(F32)).astype(BF16)

    arrived(far_n)
    relay_n = started([
        copy(far_noise.at[which[k]], near_noise.at[3 + k], SEM_RN + k, y_mates[k]) for k in range(3)
    ])

    def near_step(i, carry):
        at_rows = pl.ds(pl.multiple_of(i * OUT_ROWS, OUT_ROWS), OUT_ROWS)
        total = dot(tiles[6, at_rows, :], probe_bf[6], 1, 1)
        for c in range(3):
            total = total + dot(tiles[c, at_rows, :], probe_bf[c], 1, 1)
        totals[at_rows, :] = total
        return carry

    lax.fori_loop(0, POINTS // OUT_ROWS, near_step, 0)

    for k in (2, 0, 1):
        arrived(relay_p[k : k + 1])
        fill_right(3 + k)
        fill_tile(3 + k)
        far_probes[k] = probes_of(3 + k)
    for k in (2, 0, 1):
        arrived(relay_n[k : k + 1])
        probe_bf[3 + k] = (far_probes[k] + near_noise[3 + k].astype(F32)).astype(BF16)

    def far_step(i, carry):
        at_rows = pl.ds(pl.multiple_of(i * OUT_ROWS, OUT_ROWS), OUT_ROWS)
        total = totals[at_rows, :]
        for c in range(3, 6):
            total = total + dot(tiles[c, at_rows, :], probe_bf[c], 1, 1)
        out_t[:, at_rows] = total.T * (1.0 / 32.0) + NOISE_WEIGHT * probes_t[:, at_rows]
        return carry

    lax.fori_loop(0, POINTS // OUT_ROWS, far_step, 0)
    saves.append(save(out_t, out_hbm, 3))

    for copies in (
        core_copy, near_p, z_first, z_second, plus, far_p, cover, back, near_n, far_n, relay_p, relay_n, passed
    ):
        for one in copies:
            one.wait_send()
    for one in saves:
        one.wait()


def factor_kernel(left, pivots_right, inverse, given_t, factor, out_t):
    block = jnp.exp(dot(left[...], pivots_right[...], 1, 1))
    factor[...] = dot(block, inverse[...], 1, 1, HIGHEST)
    out_t[...] = given_t[...]


def shards(points, pivots, owners, coeffs, noise):
    vmem, smem = pl.BlockSpec(memory_space=pltpu.VMEM), pl.BlockSpec(memory_space=pltpu.SMEM)
    anywhere = pl.BlockSpec(memory_space=pl.ANY)
    block = (WIDTH, POINTS)
    part = (64, LANES)
    given_t, left, pivots_right, inverse = pl.pallas_call(
        kernel,
        out_shape=(
            jax.ShapeDtypeStruct(block, F32),
            jax.ShapeDtypeStruct((POINTS, LANES), BF16),
            jax.ShapeDtypeStruct((RANK, LANES), BF16),
            jax.ShapeDtypeStruct((RANK, RANK), F32),
        ),
        in_specs=[smem, vmem, anywhere, anywhere, anywhere],
        out_specs=(anywhere, anywhere, anywhere, anywhere),
        scratch_shapes=[
            pltpu.VMEM(block, F32),
            pltpu.VMEM((POINTS, LANES), BF16),
            pltpu.VMEM((RANK, LANES), BF16),
            pltpu.VMEM((RANK, RANK), F32),
            pltpu.VMEM(block, BF16),
            pltpu.VMEM((WIDTH, RANK), F32),
            pltpu.VMEM(block, F32),
            pltpu.VMEM(block, BF16),
            pltpu.VMEM((2,) + part, BF16),
            pltpu.VMEM(part, BF16),
            pltpu.VMEM((4,) + part, BF16),
            pltpu.VMEM((4,) + part, BF16),
            pltpu.VMEM((3,) + part, BF16),
            pltpu.VMEM((7,) + part, BF16),
            pltpu.VMEM((2,) + part, BF16),
            pltpu.VMEM((2,) + block, BF16),
            pltpu.VMEM((2,) + block, BF16),
            pltpu.VMEM((6,) + block, BF16),
            pltpu.VMEM((6,) + block, BF16),
            pltpu.VMEM((7, LANES, POINTS), BF16),
            pltpu.VMEM((7, POINTS, POINTS), BF16),
            pltpu.VMEM((7,) + block, BF16),
            pltpu.VMEM(block, F32),
            pltpu.VMEM((POINTS, WIDTH), F32),
            pltpu.VMEM((3,) + block, F32),
            pltpu.SemaphoreType.DMA((SEMS,)),
            pltpu.SemaphoreType.DMA((SEMS,)),
            pltpu.SemaphoreType.DMA((3,)),
            pltpu.SemaphoreType.DMA((4,)),
        ],
        compiler_params=pltpu.CompilerParams(
            collective_id=0, has_side_effects=True, vmem_limit_bytes=62 * 1024 * 1024
        ),
    )(owners, pivots, points.T, coeffs.T, noise.T)
    steps = 4
    tall = POINTS // steps
    factor, out_t = pl.pallas_call(
        factor_kernel,
        grid=(steps,),
        out_shape=(
            jax.ShapeDtypeStruct((POINTS, RANK), F32),
            jax.ShapeDtypeStruct(block, F32),
        ),
        in_specs=[
            pl.BlockSpec((tall, LANES), lambda i: (i, 0)),
            pl.BlockSpec((RANK, LANES), lambda i: (0, 0)),
            pl.BlockSpec((RANK, RANK), lambda i: (0, 0)),
            pl.BlockSpec((WIDTH, tall), lambda i: (0, i)),
        ],
        out_specs=(
            pl.BlockSpec((tall, RANK), lambda i: (i, 0)),
            pl.BlockSpec((WIDTH, tall), lambda i: (0, i)),
        ),
        compiler_params=pltpu.CompilerParams(vmem_limit_bytes=62 * 1024 * 1024),
    )(left, pivots_right, inverse, given_t)
    return out_t.T, factor


def solution(mesh):
    in_specs = (P(("gx", "gy"), None), P(), P(), P(), P(("gx", "gy"), None))
    out_specs = (P(("gx", "gy"), None), P(("gx", "gy"), None))
    return jax.shard_map(shards, mesh=mesh, in_specs=in_specs, out_specs=out_specs, check_vma=False)
```
